128 devices in a mesh: lat: 8 (over y, core), lon: 16 (over z, x).
Axes of the slice: x: 4, y: 4, z: 4, core: 2. Of those that a mesh axis runs over, the one named last changes fastest.
Arguments:
- lower: float32 [32, 2097152], P(None, ('lat', 'lon')), may hold values from 0.05 to 4
- upper: float32 [32, 2097152], P(None, ('lat', 'lon')), may hold values from 0.05 to 4
- old_temp: float32 [32, 2097152], P(None, ('lat', 'lon')), may hold values from -6 to 6
- atm_area: float32 [2097152], P(('lat', 'lon')), may hold values from 0.5 to 2
- pair_count: int32 [128, 10], P(('lat', 'lon')), may hold values from 0 to 4096, as said below
- cell_column: int32 [128, 10, 4096], P(('lat', 'lon')), may hold values from 0 to 16383
- exchange_cell_weight: float32 [128, 10, 4096], P(('lat', 'lon')), may hold values from 0.1 to 1
- cell_coef: float32 [128, 10, 4096], P(('lat', 'lon')), may hold values from 0.3 to 3
- cell_ocean: int32 [128, 10, 4096], P(('lat', 'lon')), may hold values from 0 to 16383
- surface_temp: float32 [2097152], P(('lat', 'lon')), may hold values from -6 to 6
- extra_warming: float32 [2097152], P(('lat', 'lon')), may hold values from -6 to 6
- response: float32 [2097152], P(('lat', 'lon')), may hold values from 0.1 to 1
- sea_mask: int32 [2097152], P(('lat', 'lon')), may hold values 0 or 1
- ocean_area: float32 [2097152], P(('lat', 'lon')), may hold values from 0.5 to 2
Outputs:
- level_warmth_new: float32 [32, 2097152], P(None, ('lat', 'lon'))
- fresh_seawater_warmth: float32 [2097152], P(('lat', 'lon'))
The draws below stay inside these ranges and needn't reach their ends.
Inputs may be any that keep to these rules, and one draw needn't show every extreme that they name: pair_count is 0 for every offset whose partner does not exist and 1 or more for every other; for every atmosphere owner the offset 4 pair (its own block) has all 4096 slots live.
All inputs are finite; a program needn't handle non-finite values. No bound on the sum of `sea_mask` on one device may be relied on, other than what follows from the above.
Results may differ from the reference program's by a relative error of at most 0.00002.
Values sent between devices are 32-bit elements; how exact they have to be, the bound alone decides.
No kernel may reach another device: no remote copies, remote signals or barrier semaphores. Data moves between devices by JAX's collectives and lax.ppermute only.
A program may use at most 128 MiB of HBM per device.

```python
import math
import jax
import jax.numpy as jnp
from jax import lax

LEV = 32
ACOL = 16384
OCEL = 16384
CAP = 128
XBLK = 32
NDEV = 128
SLOTS = 4096
NCOL = 2097152
NOCN = 2097152
N_LAT = 8
N_LON = 16


row_steps = (-1, -1, -1, 0, 0, 0, 1, 1, 1, 0)


def partner_exists(row, col, parallel_total, lon_count):
    kinds = jnp.arange(10, dtype=jnp.int32)
    row_move = jnp.array(row_steps, dtype=jnp.int32)
    partner_row_index = row[..., None] + row_move
    return (partner_row_index >= 0) & (partner_row_index < parallel_total) & ((kinds != 9) | (row[..., None] == parallel_total - 1))


def draw_pair_count(key, part):
    slot_total = XBLK * CAP
    owners = N_LAT * N_LON
    key_level, random_key_count = jax.random.split(jax.random.fold_in(key, 17), 2)
    owner = jnp.arange(owners, dtype=jnp.int32)
    exists = partner_exists(owner // N_LON, owner % N_LON, N_LAT, N_LON)
    level = jax.random.randint(key_level, (owners, 1), 1, 9)
    lowest = jnp.maximum(level * slot_total // 16, 1)
    highest = jnp.maximum(level * slot_total // 8, lowest)
    spread = jax.random.randint(random_key_count, (owners, 10), 0, 1 << 20)
    base = lowest + spread % (highest - lowest + 1)
    own = jnp.arange(10)[None, :] == 4
    counts = jnp.where(own, slot_total, base)
    return jnp.where(exists, counts, 0).astype(jnp.int32)


def place_ends(drawn, key, low, largest):
    index_at = [jax.random.randint(jax.random.fold_in(key, axis), (), 0, length) for axis, length in enumerate(drawn.shape)]
    widest = drawn.shape.index(max(drawn.shape))
    beside = index_at[:widest] + [(index_at[widest] + 1) % drawn.shape[widest]] + index_at[widest + 1:]
    return drawn.at[tuple(index_at)].set(low).at[tuple(beside)].set(largest)


def levels(stream_key, dims, pieces, least, high):
    loudness = 1.0
    for axis_at, parts in pieces:
        heights = jax.random.uniform(jax.random.fold_in(jax.random.fold_in(stream_key, 6), axis_at), (parts,), jnp.float32, least / len(pieces), high / len(pieces))
        loudness = loudness * jnp.repeat(jnp.exp(heights), dims[axis_at] // parts).reshape((-1,) + (1,) * (len(dims) - 1 - axis_at))
    return loudness


def centred(key, extent, deviation, most, pieces=(), kind=jnp.bfloat16):
    factor_of = levels(key, extent, pieces, -0.22, 0.18) if pieces else 1.0
    values = jax.random.normal(key, extent, jnp.float32) * deviation * factor_of
    return jnp.minimum(jnp.maximum(values, -most), most).astype(kind)


def setup_inputs(seed: int = 0) -> dict:
    key_of = jax.random.split(jax.random.key(seed), 15)
    return {
        "lower": jnp.clip(jnp.exp(math.log(4.0) - 4.3820266 * jax.random.uniform(key_of[0], (LEV, NCOL), jnp.float32) ** levels(key_of[0], (LEV, NCOL), ((1, 128),), -0.2, 0.2)), 0.05, 4.0),
        "upper": jnp.clip(jnp.exp(math.log(4.0) - 4.3820266 * jax.random.uniform(key_of[1], (LEV, NCOL), jnp.float32) ** levels(key_of[1], (LEV, NCOL), ((1, 128),), -0.2, 0.2)), 0.05, 4.0),
        "old_temp": centred(key_of[2], (LEV, NCOL), 1.0, 6.0, ((1, 128),), jnp.float32),
        "atm_area": jnp.clip(jnp.exp(math.log(2.0) - 1.3862944 * jax.random.uniform(key_of[3], (NCOL,), jnp.float32) ** levels(key_of[3], (NCOL,), ((0, 128),), -0.2, 0.2)), 0.5, 2.0),
        "pair_count": draw_pair_count(jax.random.fold_in(key_of[14], 71), 0),
        "cell_column": place_ends(jax.random.randint(key_of[5], (NDEV, 10, SLOTS), 0, ACOL), jax.random.fold_in(key_of[5], 1), 0, ACOL - 1).astype(jnp.int32),
        "exchange_cell_weight": jnp.clip(jnp.exp(math.log(1.0) - 2.3025851 * jax.random.uniform(key_of[6], (NDEV, 10, SLOTS), jnp.float32) ** levels(key_of[6], (NDEV, 10, SLOTS), ((0, 128),), -0.2, 0.2)), 0.1, 1.0),
        "cell_coef": jnp.clip(jnp.exp(math.log(3.0) - 2.3025851 * jax.random.uniform(key_of[7], (NDEV, 10, SLOTS), jnp.float32) ** levels(key_of[7], (NDEV, 10, SLOTS), ((0, 128),), -0.2, 0.2)), 0.3, 3.0),
        "cell_ocean": place_ends(jax.random.randint(key_of[8], (NDEV, 10, SLOTS), 0, OCEL), jax.random.fold_in(key_of[8], 1), 0, OCEL - 1).astype(jnp.int32),
        "surface_temp": centred(key_of[9], (NOCN,), 1.0, 6.0, ((0, 128),), jnp.float32),
        "extra_warming": centred(key_of[10], (NOCN,), 1.0, 6.0, ((0, 128),), jnp.float32),
        "response": jnp.clip(jnp.exp(math.log(1.0) - 2.3025851 * jax.random.uniform(key_of[11], (NOCN,), jnp.float32) ** levels(key_of[11], (NOCN,), ((0, 128),), -0.2, 0.2)), 0.1, 1.0),
        "sea_mask": place_ends((jax.random.randint(key_of[12], (NOCN,), 0, 4) < 3).astype(jnp.int32), jax.random.fold_in(key_of[12], 1), 0, 1),
        "ocean_area": jnp.clip(jnp.exp(math.log(2.0) - 1.3862944 * jax.random.uniform(key_of[13], (NOCN,), jnp.float32) ** levels(key_of[13], (NOCN,), ((0, 128),), -0.2, 0.2)), 0.5, 2.0),
    }


row_steps = (-1, -1, -1, 0, 0, 0, 1, 1, 1, 0)
column_hops = (-1, 0, 1, -1, 0, 1, -1, 0, 1, 0)


def partners(row, col, parallel_total, lon_count, sign):
    kinds = jnp.arange(10, dtype=jnp.int32)
    row_move = jnp.array(row_steps, dtype=jnp.int32)
    col_move = jnp.where(kinds == 9, jnp.int32(lon_count // 2), jnp.array(column_hops, dtype=jnp.int32)).astype(jnp.int32)
    partner_row_index = row[..., None] + sign * row_move
    other_col = jnp.mod(col[..., None] + sign * col_move, lon_count)
    exists = (partner_row_index >= 0) & (partner_row_index < parallel_total) & ((kinds != 9) | (row[..., None] == parallel_total - 1))
    return (partner_row_index * lon_count + other_col).astype(jnp.int32), exists


def sweep_down(carry, inputs):
    e_above, g_above = carry
    low, up, rhs = inputs
    den = 1.0 + low + up - up * g_above
    e_here = (rhs + up * e_above) / den
    g_here = low / den
    return (e_here, g_here), (e_here, g_here)


def sweep_up(below, inputs):
    e_here, g_here = inputs
    value = e_here + g_here * below
    return value, value


def reference(lower, upper, old_temp, atm_area, pair_count, cell_column, exchange_cell_weight, cell_coef, cell_ocean, surface_temp, extra_warming, response, sea_mask, ocean_area):
    ncols = lower.shape[1]
    zeros = jnp.zeros((ncols,), lower.dtype)
    (e_one, g_one), (e_all, g_all) = lax.scan(sweep_down, (zeros, zeros), (lower[1:], upper[1:], old_temp[1:]), reverse=True)
    den_low = 1.0 + lower[0] + upper[0] - upper[0] * g_one
    e_low = (old_temp[0] + upper[0] * e_one) / den_low
    f_low = 1.0 / den_low
    gsea = response * sea_mask.astype(response.dtype)
    target = surface_temp + gsea * extra_warming
    owner = jnp.arange(NDEV, dtype=jnp.int32)
    partner, exists = partners(owner // N_LON, owner % N_LON, N_LAT, N_LON, 1)
    safe = jnp.where(exists, partner, jnp.int32(0)).astype(jnp.int32)
    kinds = jnp.arange(10, dtype=jnp.int32)
    ocean_at = safe[:, :, None] * OCEL + cell_ocean[safe, kinds[None, :]]
    col_global = owner[:, None, None] * ACOL + cell_column
    flux = cell_coef * (target[ocean_at] - e_low[col_global]) / (1.0 + cell_coef * (gsea[ocean_at] + f_low[col_global]))
    live = jnp.arange(SLOTS, dtype=jnp.int32)[None, None, :] < pair_count[:, :, None]
    weighted = jnp.where(live, exchange_cell_weight * flux, jnp.zeros_like(flux))
    atm_flux = jax.ops.segment_sum(weighted.reshape(-1), col_global.reshape(-1), num_segments=ncols) / atm_area
    ocean_flux = jax.ops.segment_sum(weighted.reshape(-1), ocean_at.reshape(-1), num_segments=surface_temp.shape[0]) / ocean_area
    fresh_seawater_warmth = surface_temp + gsea * (extra_warming - ocean_flux)
    bottom_stratum = e_low + f_low * atm_flux
    _, leftover_patches = lax.scan(sweep_up, bottom_stratum, (e_all, g_all))
    level_warmth_new = jnp.concatenate([bottom_stratum[None], leftover_patches], axis=0)
    return (level_warmth_new, fresh_seawater_warmth)
```

```python
import functools

import jax
import jax.numpy as jnp
from jax import lax
from jax.experimental import pallas as pl
from jax.experimental.pallas import tpu as pltpu
from jax.sharding import PartitionSpec as P

F32 = jnp.float32
BF16 = jnp.bfloat16
ROWS = 32
STEP = 8
LEVELS = 32
VMEM = pl.BlockSpec(memory_space=pltpu.VMEM)
SMEM = pl.BlockSpec(memory_space=pltpu.SMEM)


def slot_kind(slot, row, ocean):
    odd = lax.rem(row, 2) == 1
    if slot < 3:
        first = jnp.where(odd, 6, 0) if ocean else jnp.where(odd, 0, 6)
        return first + slot, True
    if slot < 6:
        first = jnp.where(odd, 0, 6) if ocean else jnp.where(odd, 6, 0)
        kind = first + slot - 3
        if slot == 4:
            return jnp.where(row == 7, 9, kind), row > 0
        return kind, (row > 0) & (row < 7)
    return {6: 3, 7: 5, 8: 4}[slot], True


def two_terms(x):
    high = x.astype(BF16)
    return high, (x - high.astype(F32)).astype(BF16)


def fill_table(table_ref, fields):
    for t, field in enumerate(fields):
        for p, term in enumerate(two_terms(field)):
            table_ref[pl.ds(t * 128 + p * 64, 64), 0:128] = term[0:64]
            table_ref[pl.ds(t * 128 + p * 64, 64), 128:256] = term[64:128]


def gather_chunk(table_ref, idx, store):
    iota_k = lax.broadcasted_iota(jnp.int32, (256, 128), 0).astype(F32).astype(BF16)
    iota_m = lax.broadcasted_iota(jnp.int32, (64, 128), 0)
    k = ((idx & 127) | ((idx >> 13) << 7)).astype(F32)
    m = (idx >> 7) & 63
    one, zero = jnp.ones((), BF16), jnp.zeros((), BF16)
    for h in range(0, STEP, 2):
        hot = jnp.concatenate(
            [
                jnp.where(
                    iota_k == jnp.broadcast_to(k[r : r + 1], (256, 128)).astype(BF16), one, zero
                )
                for r in (h, h + 1)
            ],
            axis=1,
        )
        found = jnp.dot(table_ref[...], hot, preferred_element_type=F32)
        for r in (h, h + 1):
            mask = iota_m == jnp.broadcast_to(m[r : r + 1], (64, 128))
            cols = slice((r - h) * 128, (r - h + 1) * 128)
            for t in range(2):
                both = found[t * 128 : t * 128 + 64, cols] + found[t * 128 + 64 : t * 128 + 128, cols]
                store(t, r, jnp.sum(jnp.where(mask, both, 0.0), axis=0, keepdims=True))


def add_chunk(acc_ref, idx, value):
    iota = lax.broadcasted_iota(jnp.int32, (128, 128), 0).astype(F32).astype(BF16)
    one, zero = jnp.ones((), BF16), jnp.zeros((), BF16)
    low = (idx & 127).astype(F32)
    high = (idx >> 7).astype(F32)
    first = value.astype(BF16).astype(F32)
    second = value - first
    left, right0, right1 = [], [], []
    for r in range(idx.shape[0]):
        spread = lambda x: jnp.broadcast_to(x[r : r + 1], (128, 128)).astype(BF16)
        left.append(jnp.where(iota == spread(high), one, zero))
        mask = iota == spread(low)
        right0.append(jnp.where(mask, spread(first), zero))
        right1.append(jnp.where(mask, spread(second), zero))
    left = jnp.concatenate(left, axis=1)
    right = jnp.concatenate(
        [jnp.concatenate(right0, axis=1), jnp.concatenate(right1, axis=1)], axis=0
    )
    acc_ref[...] += lax.dot_general(left, right, (((1,), (1,)), ((), ())), preferred_element_type=F32)


def chunks(count):
    return lax.div(count + (STEP * 128 - 1), STEP * 128)


def rows_at(start):
    return pl.ds(pl.multiple_of(start, STEP), STEP)


def ocean_states(temp_ref, warm_ref, resp_ref, mask_ref):
    gsea = resp_ref[...] * mask_ref[...].astype(F32)
    return temp_ref[...] + gsea * warm_ref[...], gsea


def ocean_gather_kernel(temp_ref, warm_ref, resp_ref, mask_ref, idx_ref, a_ref, b_ref, c_ref, table_ref):
    row = lax.axis_index("lat")
    fill_table(table_ref, ocean_states(temp_ref, warm_ref, resp_ref, mask_ref))
    places = [(a_ref, 0), (a_ref, 1), (a_ref, 2), (b_ref, 0), (b_ref, 1), (b_ref, 2), (c_ref, 0), (c_ref, 1)]
    for slot, (out_ref, at) in enumerate(places):
        kind, exists = slot_kind(slot, row, True)

        def body(n, _):
            def store(t, r, values):
                out_ref[at, t, pl.ds(n * STEP + r, 1), :] = values

            gather_chunk(table_ref, idx_ref[rows_at(kind * ROWS + n * STEP), :], store)
            return 0

        lax.fori_loop(0, jnp.where(exists, ROWS // STEP, 0), body, 0)


def sweep_down_kernel(low_ref, up_ref, old_ref, e_ref, g_ref, f_ref):
    width = e_ref.shape[1]
    e = [jnp.zeros((8, 128), F32) for _ in range(width // 8)]
    g = [jnp.zeros((8, 128), F32) for _ in range(width // 8)]
    for level in range(LEVELS - 1, -1, -1):
        i, s = divmod(level, 8)
        for v in range(width // 8):
            at = pl.ds(v * 64 + s, 8, stride=8)
            low, up, old = low_ref[i, at, :], up_ref[i, at, :], old_ref[i, at, :]
            inverse = 1.0 / (1.0 + low + up - up * g[v])
            e[v] = (old + up * e[v]) * inverse
            e_ref[level, pl.ds(v * 8, 8), :] = e[v]
            if level:
                g[v] = low * inverse
                g_ref[level, pl.ds(v * 8, 8), :] = g[v]
            else:
                f_ref[pl.ds(v * 8, 8), :] = inverse


def own_gather_kernel(temp_ref, warm_ref, resp_ref, mask_ref, idx_ref, d_ref, table_ref):
    fill_table(table_ref, ocean_states(temp_ref, warm_ref, resp_ref, mask_ref))

    def body(n, _):
        def store(t, r, values):
            d_ref[t, pl.ds(n * STEP + r, 1), :] = values

        gather_chunk(table_ref, idx_ref[rows_at(4 * ROWS + n * STEP), :], store)
        return 0

    lax.fori_loop(0, ROWS // STEP, body, 0)


def column_gather_kernel(count_ref, e_ref, f_ref, idx_ref, out_ref, table_ref):
    row = lax.axis_index("lat")
    fill_table(table_ref, (e_ref[0], f_ref[...]))
    for slot in range(9):
        kind, exists = slot_kind(slot, row, False)

        def body(n, _):
            def store(t, r, values):
                out_ref[t, slot, pl.ds(n * STEP + r, 1), :] = values

            gather_chunk(table_ref, idx_ref[rows_at(kind * ROWS + n * STEP), :], store)
            return 0

        lax.fori_loop(0, jnp.where(exists, chunks(count_ref[0, kind]), 0), body, 0)


def flux_kernel(
    count_ref, minus_ref, plus_ref, a_ref, b_ref, d_ref, column_ref, coef_ref, weight_ref,
    minus_out, plus_out, mid_out,
):
    row = lax.axis_index("lat")
    places = [
        (minus_ref, 0, minus_out, 0), (a_ref, 1, mid_out, 0), (plus_ref, 0, plus_out, 0),
        (minus_ref, 1, minus_out, 1), (b_ref, 1, mid_out, 1), (plus_ref, 1, plus_out, 1),
        (minus_ref, 2, minus_out, 2), (plus_ref, 2, plus_out, 2), (d_ref, None, mid_out, 2),
    ]
    place = lax.broadcasted_iota(jnp.int32, (ROWS, 128), 0) * 128 + lax.broadcasted_iota(
        jnp.int32, (ROWS, 128), 1
    )
    for slot, (in_ref, at, out_ref, to) in enumerate(places):
        kind, exists = slot_kind(slot, row, False)
        count = jnp.where(exists, count_ref[0, kind], 0)
        rows = pl.ds(pl.multiple_of(kind * ROWS, ROWS), ROWS)
        target, gsea = (in_ref[0], in_ref[1]) if at is None else (in_ref[at, 0], in_ref[at, 1])
        coef = coef_ref[rows, :]
        flux = coef * (target - column_ref[0, slot]) / (1.0 + coef * (gsea + column_ref[1, slot]))
        out_ref[to] = jnp.where(place < count, weight_ref[rows, :] * flux, 0.0)


def column_scatter_kernel(count_ref, minus_ref, plus_ref, mid_ref, idx_ref, out_ref, acc_ref):
    row = lax.axis_index("lat")
    acc_ref[...] = jnp.zeros_like(acc_ref)
    places = [
        (minus_ref, 0), (mid_ref, 0), (plus_ref, 0), (minus_ref, 1), (mid_ref, 1), (plus_ref, 1),
        (minus_ref, 2), (plus_ref, 2), (mid_ref, 2),
    ]
    for slot, (in_ref, at) in enumerate(places):
        kind, exists = slot_kind(slot, row, False)

        def body(n, _):
            add_chunk(acc_ref, idx_ref[rows_at(kind * ROWS + n * STEP), :], in_ref[at, rows_at(n * STEP), :])
            return 0

        lax.fori_loop(0, jnp.where(exists, chunks(count_ref[0, kind]), 0), body, 0)
    out_ref[...] = acc_ref[:, 0:128] + acc_ref[:, 128:256]


def sweep_up_kernel(sum_ref, area_ref, e_ref, g_ref, f_ref, out_ref):
    width = e_ref.shape[1]
    for v in range(width // 8):
        rows = pl.ds(v * 8, 8)
        value = e_ref[0, rows, :] + f_ref[rows, :] * (sum_ref[rows, :] / area_ref[rows, :])
        out_ref[0, pl.ds(v * 64, 8, stride=8), :] = value
        for level in range(1, LEVELS):
            i, s = divmod(level, 8)
            value = e_ref[level, rows, :] + g_ref[level, rows, :] * value
            out_ref[i, pl.ds(v * 64 + s, 8, stride=8), :] = value


def own_scatter_kernel(mid_ref, idx_ref, out_ref):
    out_ref[...] = jnp.zeros_like(out_ref)

    def body(n, _):
        add_chunk(out_ref, idx_ref[rows_at(4 * ROWS + n * STEP), :], mid_ref[2, rows_at(n * STEP), :])
        return 0

    lax.fori_loop(0, ROWS // STEP, body, 0)


def ocean_scatter_kernel(
    own_ref, a_ref, b_ref, minus_ref, plus_ref, idx_ref, temp_ref, warm_ref, resp_ref, mask_ref, area_ref,
    out_ref, acc_ref,
):
    row = lax.axis_index("lat")
    acc_ref[...] = own_ref[...]
    places = [(a_ref, 0), (a_ref, 1), (a_ref, 2), (b_ref, 0), (b_ref, 1), (b_ref, 2), (minus_ref, 2), (plus_ref, 2)]
    for slot, (in_ref, at) in enumerate(places):
        kind, exists = slot_kind(slot, row, True)

        def body(n, _):
            add_chunk(acc_ref, idx_ref[rows_at(kind * ROWS + n * STEP), :], in_ref[at, rows_at(n * STEP), :])
            return 0

        lax.fori_loop(0, jnp.where(exists, ROWS // STEP, 0), body, 0)
    flux = (acc_ref[:, 0:128] + acc_ref[:, 128:256]) / area_ref[...]
    gsea = resp_ref[...] * mask_ref[...].astype(F32)
    out_ref[...] = temp_ref[...] + gsea * (warm_ref[...] - flux)


def to_tiles(x):
    return x.reshape(4, 8, 128, 128).transpose(0, 2, 1, 3).reshape(4, 1024, 128)


def from_tiles(x):
    return x.reshape(4, 128, 8, 128).transpose(0, 2, 1, 3).reshape(LEVELS, 16384)


def shape(*dims, dtype=F32):
    return jax.ShapeDtypeStruct(dims, dtype)


BOTH = ("lat", "lon")


def swap_rows(x):
    return lax.ppermute(x, BOTH, [(i * 16 + j, (i ^ 1) * 16 + j) for i in range(8) for j in range(16)])


def outer_rows(x):
    pairs = []
    for i in range(8):
        to = i + 1 if i % 2 else i - 1
        for j in range(16):
            if 0 <= to < 8:
                pairs.append((i * 16 + j, to * 16 + j))
            elif i == 7:
                pairs.append((i * 16 + j, i * 16 + (j + 8) % 16))
    return lax.ppermute(x, BOTH, pairs)


def along_row(x, hop):
    return lax.ppermute(x, "lon", [(j, (j + hop) % 16) for j in range(16)])


def on_device(
    lower, upper, old_temp, atm_area, pair_count, cell_column, exchange_cell_weight, cell_coef, cell_ocean,
    surface_temp, extra_warming, response, sea_mask, ocean_area,
):
    square = lambda x: x.reshape(128, 128)
    cells = lambda x: x.reshape(10 * ROWS, 128)
    ocean = [square(x) for x in (surface_temp, extra_warming, response, sea_mask)]
    columns, weight, coef, cell_ocean = map(cells, (cell_column, exchange_cell_weight, cell_coef, cell_ocean))
    table = pltpu.VMEM((256, 256), BF16)
    acc = pltpu.VMEM((128, 256), F32)

    a, b, c = pl.pallas_call(
        ocean_gather_kernel,
        out_shape=(shape(3, 2, ROWS, 128), shape(3, 2, ROWS, 128), shape(2, 2, ROWS, 128)),
        in_specs=[VMEM] * 5,
        out_specs=(VMEM,) * 3,
        scratch_shapes=[table],
        name="ocean_gather",
    )(*ocean, cell_ocean)
    a = swap_rows(a)
    b = outer_rows(b)

    width = 64
    tiles = pl.BlockSpec((4, width * 8, 128), lambda n: (0, n, 0))
    levels = pl.BlockSpec((LEVELS, width, 128), lambda n: (0, n, 0))
    plane = pl.BlockSpec((width, 128), lambda n: (n, 0))
    e, g, f = pl.pallas_call(
        sweep_down_kernel,
        grid=(128 // width,),
        out_shape=(shape(LEVELS, 128, 128), shape(LEVELS, 128, 128), shape(128, 128)),
        in_specs=[tiles] * 3,
        out_specs=(levels, levels, plane),
        name="sweep_down",
    )(to_tiles(lower), to_tiles(upper), to_tiles(old_temp))

    minus = along_row(jnp.stack([a[0], b[0], c[0]]), 1)
    plus = along_row(jnp.stack([a[2], b[2], c[1]]), -1)

    own = pl.pallas_call(
        own_gather_kernel,
        out_shape=shape(2, ROWS, 128),
        in_specs=[VMEM] * 5,
        out_specs=VMEM,
        scratch_shapes=[table],
        name="own_gather",
    )(*ocean, cell_ocean)
    at_columns = pl.pallas_call(
        column_gather_kernel,
        grid=(1,),
        out_shape=shape(2, 9, ROWS, 128),
        in_specs=[SMEM, pl.BlockSpec((1, 128, 128), lambda n: (0, 0, 0)), VMEM, VMEM],
        out_specs=VMEM,
        scratch_shapes=[table],
        name="column_gather",
    )(pair_count, e, f, columns)

    minus, plus, mid = pl.pallas_call(
        flux_kernel,
        out_shape=(shape(3, ROWS, 128),) * 3,
        in_specs=[SMEM] + [VMEM] * 8,
        out_specs=(VMEM,) * 3,
        name="flux",
    )(pair_count, minus, plus, a, b, own, at_columns, coef, weight)
    back_minus = along_row(minus, -1)
    back_plus = along_row(plus, 1)

    column_sum = pl.pallas_call(
        column_scatter_kernel,
        out_shape=shape(128, 128),
        in_specs=[SMEM] + [VMEM] * 4,
        out_specs=VMEM,
        scratch_shapes=[acc],
        name="column_scatter",
    )(pair_count, minus, plus, mid, columns)

    back_a = swap_rows(jnp.stack([back_minus[0], mid[0], back_plus[0]]))
    back_b = outer_rows(jnp.stack([back_minus[1], mid[1], back_plus[1]]))

    level_warmth_new = pl.pallas_call(
        sweep_up_kernel,
        grid=(128 // width,),
        out_shape=shape(4, 1024, 128),
        in_specs=[plane, plane, levels, levels, plane],
        out_specs=tiles,
        name="sweep_up",
    )(column_sum, square(atm_area), e, g, f)
    own_sum = pl.pallas_call(
        own_scatter_kernel,
        out_shape=shape(128, 256),
        in_specs=[VMEM] * 2,
        out_specs=VMEM,
        name="own_scatter",
    )(mid, cell_ocean)
    fresh_seawater_warmth = pl.pallas_call(
        ocean_scatter_kernel,
        out_shape=shape(128, 128),
        in_specs=[VMEM] * 11,
        out_specs=VMEM,
        scratch_shapes=[acc],
        name="ocean_scatter",
    )(own_sum, back_a, back_b, back_minus, back_plus, cell_ocean, *ocean, square(ocean_area))
    return from_tiles(level_warmth_new), fresh_seawater_warmth.reshape(16384)


def solution(mesh):
    owners = ("lat", "lon")
    wide, flat = P(None, owners), P(owners)
    lists = P(owners, None, None)
    return jax.shard_map(
        on_device,
        mesh=mesh,
        in_specs=(wide, wide, wide, flat, P(owners, None), lists, lists, lists, lists) + (flat,) * 5,
        out_specs=(wide, flat),
        check_vma=False,
    )
```

```python
import functools

import jax
import jax.numpy as jnp
from jax import lax
from jax.experimental import pallas as pl
from jax.experimental.pallas import tpu as pltpu
from jax.sharding import PartitionSpec as P

F32 = jnp.float32
BF16 = jnp.bfloat16
ROWS = 32
STEP = 8
CHUNKS = ROWS // STEP
UNROLL = 4
LEVELS = 32
SPARE = 9 * ROWS
VMEM = pl.BlockSpec(memory_space=pltpu.VMEM)
SMEM = pl.BlockSpec(memory_space=pltpu.SMEM)
HBM = pl.BlockSpec(memory_space=pltpu.HBM)

SLOTS = ("A-", "B-", "C-", "A+", "B+", "C+", "A0", "B0", "C0")
SENT = ("A-", "A0", "A+", "B-", "B0", "B+", "C-", "C+", "C0")


def slot_kind(slot, row, ocean):
    hop = "-0+".index(slot[1])
    if slot[0] == "C":
        return 3 + hop, True
    below = (lax.rem(row, 2) == 1) == (ocean == (slot[0] == "A"))
    kind = jnp.where(below, 6, 0) + hop
    if slot[0] == "A":
        return kind, True
    if hop == 1:
        return jnp.where(row == 7, 9, kind), row > 0
    return kind, (row > 0) & (row < 7)


def list_chunks(from_ref, to_ref, row, ocean, place, spare, count_ref=None, slots=SLOTS):
    total = jnp.int32(0)
    for slot in slots:
        kind, exists = slot_kind(slot, row, ocean)
        number = CHUNKS
        if count_ref is not None:
            number = lax.div(count_ref[0, kind] + (STEP * 128 - 1), STEP * 128)
        for c in range(CHUNKS):
            from_ref[total + c] = kind * ROWS + c * STEP
            to_ref[total + c] = place(slot) + c * STEP
        total = total + jnp.where(exists, number, 0)
    for c in range(2 * UNROLL):
        from_ref[total + c] = jnp.int32(0)
        to_ref[total + c] = jnp.int32(spare)
    return total


LIST = [pltpu.SMEM((9 * CHUNKS + 2 * UNROLL,), jnp.int32)] * 2
TRIPS = lambda total: lax.div(total + (UNROLL - 1), UNROLL)


def rows_at(start):
    return pl.ds(pl.multiple_of(start, STEP), STEP)


def spread(x, r, n):
    return jnp.broadcast_to(x[r : r + 1], (n, 128))


def two_terms(x):
    high = x.astype(BF16)
    return high, (x - high.astype(F32)).astype(BF16)


def fill_table(table_ref, fields):
    for t, field in enumerate(fields):
        for p, term in enumerate(two_terms(field)):
            table_ref[p, pl.ds(t * 64, 64), 0:128] = term[0:64]
            table_ref[p, pl.ds(t * 64, 64), 128:256] = term[64:128]


def look_up(table_ref, idx, accs, iota):
    k = ((idx & 127) | ((idx >> 13) << 7)).astype(F32)
    one, zero = jnp.ones((), BF16), jnp.zeros((), BF16)
    for h, acc in enumerate(accs):
        hot = [jnp.where(iota == spread(k, r, 256).astype(BF16), one, zero) for r in (2 * h, 2 * h + 1)]
        pltpu.matmul_push_rhs(jnp.concatenate(hot, axis=1), h // 2, h % 2)
        pltpu.matmul_acc_lhs(acc, table_ref[0], load_staged_rhs=h // 2)
        pltpu.matmul_acc_lhs(acc, table_ref[1])


def pick(idx, accs):
    group, place = (idx >> 10) & 7, (idx >> 7) & 7
    iota = lax.broadcasted_iota(jnp.int32, (8, 128), 0)
    values = [None, None]
    for h, acc in enumerate(accs):
        found = pltpu.matmul_pop(acc)
        for r in range(2):
            row, cols = 2 * h + r, slice(r * 128, r * 128 + 128)
            here = spread(group, row, 8)
            for t in range(2):
                eight = found[t * 64 : t * 64 + 8, cols]
                for j in range(1, 8):
                    eight = jnp.where(here == j, found[t * 64 + 8 * j : t * 64 + 8 * j + 8, cols], eight)
                value = jnp.take_along_axis(eight, spread(place, row, 8), axis=0)
                values[t] = value if row == 0 else jnp.where(iota == row, value, values[t])
    return values


def gather(table_ref, idx_ref, out_ref, apart, from_ref, to_ref, total):
    def run(*accs):
        iota = lax.broadcasted_iota(jnp.int32, (256, 128), 0).astype(F32).astype(BF16)
        sets = accs[:4], accs[4:]
        read = lambda n: idx_ref[rows_at(from_ref[n]), :]

        def finish(n, which):
            for t, value in enumerate(pick(read(n), sets[which])):
                out_ref[rows_at(to_ref[n] + t * apart), :] = value

        look_up(table_ref, read(0), sets[0], iota)

        def body(trip, _):
            for u in range(UNROLL):
                n = trip * UNROLL + u
                look_up(table_ref, read(n + 1), sets[(u + 1) % 2], iota)
                finish(n, u % 2)
            return 0

        lax.fori_loop(0, TRIPS(total), body, 0)
        for acc in sets[0]:
            pltpu.matmul_pop(acc)

    pl.run_scoped(run, *[pltpu.ACC(h % 2)((128, 256), F32) for _ in range(2) for h in range(4)])


def scatter(idx_ref, value_ref, from_ref, to_ref, total):
    def run(acc0, acc1):
        accs = acc0, acc1
        iota = lax.broadcasted_iota(jnp.int32, (128, 128), 0).astype(F32).astype(BF16)
        one, zero = jnp.ones((), BF16), jnp.zeros((), BF16)

        def body(trip, _):
            for u in range(UNROLL):
                n = trip * UNROLL + u
                idx = idx_ref[rows_at(from_ref[n]), :]
                value = value_ref[rows_at(to_ref[n]), :]
                low, high = (idx & 127).astype(F32), (idx >> 7).astype(F32)
                first = value.astype(BF16).astype(F32)
                second = value - first
                for h in range(4):
                    left, right = [], [[], []]
                    for r in (2 * h, 2 * h + 1):
                        at = lambda x: spread(x, r, 128).astype(BF16)
                        left.append(jnp.where(iota == at(high), one, zero))
                        mask = iota == at(low)
                        right[0].append(jnp.where(mask, at(first), zero))
                        right[1].append(jnp.where(mask, at(second), zero))
                    right = jnp.concatenate([jnp.concatenate(x, axis=1) for x in right], axis=0)
                    pltpu.matmul_push_rhs(right, h // 2, h % 2, transpose=True)
                    pltpu.matmul_acc_lhs(accs[h % 2], jnp.concatenate(left, axis=1), load_staged_rhs=h // 2)
            return 0

        lax.fori_loop(0, TRIPS(total), body, 0)
        both = pltpu.matmul_pop(acc0) + pltpu.matmul_pop(acc1)
        return both[:, 0:128] + both[:, 128:256]

    return pl.run_scoped(run, *[pltpu.ACC(m)((128, 256), F32) for m in range(2)])


def ocean_gather_kernel(*refs):
    count = (len(refs) - 5) // 2
    sources, kept = refs[:count], refs[count : 2 * count]
    out_ref, table_ref, from_ref, to_ref, sems = refs[2 * count :]
    copies = [pltpu.make_async_copy(x, y, sems.at[n]) for n, (x, y) in enumerate(zip(sources, kept))]
    for copy in copies:
        copy.start()
    row = lax.axis_index("lat")
    place = lambda slot: SENT.index(slot) * 2 * ROWS
    total = list_chunks(from_ref, to_ref, row, True, place, 2 * SPARE, slots=SLOTS[:-1])
    for copy in copies[:5]:
        copy.wait()
    temp_ref, warm_ref, resp_ref, mask_ref, idx_ref = kept[:5]
    fill_table(table_ref, ocean_states(temp_ref, warm_ref, resp_ref, mask_ref))
    gather(table_ref, idx_ref, out_ref, ROWS, from_ref, to_ref, total)
    for copy in copies[5:]:
        copy.wait()


def ocean_states(temp_ref, warm_ref, resp_ref, mask_ref):
    gsea = resp_ref[...] * mask_ref[...].astype(F32)
    return temp_ref[...] + gsea * warm_ref[...], gsea


def sweep_down_kernel(
    low_ref, up_ref, old_ref, temp_ref, warm_ref, resp_ref, mask_ref, idx_ref,
    e_ref, g_ref, f_ref, own_ref, table_ref, from_ref, to_ref,
):
    def half(n, _):
        e = [jnp.zeros((8, 128), F32) for _ in range(8)]
        g = [jnp.zeros((8, 128), F32) for _ in range(8)]
        for level in range(LEVELS - 1, -1, -1):
            i, s = divmod(level, 8)
            for v in range(8):
                at = pl.ds(n * 512 + v * 64 + s, 8, stride=8)
                to = rows_at(n * 64 + v * 8)
                low, up, old = low_ref[i, at, :], up_ref[i, at, :], old_ref[i, at, :]
                inverse = 1.0 / (1.0 + low + up - up * g[v])
                e[v] = (old + up * e[v]) * inverse
                e_ref[level, to, :] = e[v]
                if level:
                    g[v] = low * inverse
                    g_ref[level, to, :] = g[v]
                else:
                    f_ref[to, :] = inverse
        return 0

    lax.fori_loop(0, 2, half, 0)
    fill_table(table_ref, ocean_states(temp_ref, warm_ref, resp_ref, mask_ref))
    total = list_chunks(from_ref, to_ref, 0, True, lambda slot: 0, 2 * ROWS, slots=SLOTS[-1:])
    gather(table_ref, idx_ref, own_ref, ROWS, from_ref, to_ref, total)


def column_gather_kernel(count_ref, e_ref, f_ref, idx_ref, out_ref, table_ref, from_ref, to_ref):
    row = lax.axis_index("lat")
    fill_table(table_ref, (e_ref[0], f_ref[...]))
    place = lambda slot: SLOTS.index(slot) * ROWS
    total = list_chunks(from_ref, to_ref, row, False, place, SPARE, count_ref)
    gather(table_ref, idx_ref, out_ref, SPARE + STEP, from_ref, to_ref, total)


def flux_kernel(count_ref, minus_ref, plus_ref, a_ref, b_ref, own_ref, column_ref, coef_ref, weight_ref, out_ref):
    row = lax.axis_index("lat")
    places = {"A0": (a_ref, 1), "B0": (b_ref, 1)}
    for n, side in enumerate("ABC"):
        places[side + "-"] = minus_ref, n
        places[side + "+"] = plus_ref, n
    order = lax.broadcasted_iota(jnp.int32, (ROWS, 128), 0) * 128 + lax.broadcasted_iota(
        jnp.int32, (ROWS, 128), 1
    )
    for n, slot in enumerate(SLOTS):
        if slot == "C0":
            target, gsea = own_ref[pl.ds(0, ROWS), :], own_ref[pl.ds(ROWS, ROWS), :]
        else:
            in_ref, at = places[slot]
            target, gsea = in_ref[at, 0], in_ref[at, 1]
        kind, exists = slot_kind(slot, row, False)
        count = jnp.where(exists, count_ref[0, kind], 0)
        rows = pl.ds(pl.multiple_of(kind * ROWS, ROWS), ROWS)
        here = pl.ds(n * ROWS, ROWS)
        coef = coef_ref[rows, :]
        e, f = column_ref[here, :], column_ref[pl.ds(SPARE + STEP + n * ROWS, ROWS), :]
        flux = coef * (target - e) / (1.0 + coef * (gsea + f))
        out_ref[here, :] = jnp.where(order < count, weight_ref[rows, :] * flux, 0.0)
    out_ref[pl.ds(SPARE, STEP), :] = jnp.zeros((STEP, 128), F32)


def column_scatter_kernel(count_ref, value_ref, idx_ref, out_ref, from_ref, to_ref):
    row = lax.axis_index("lat")
    place = lambda slot: SLOTS.index(slot) * ROWS
    total = list_chunks(from_ref, to_ref, row, False, place, SPARE, count_ref)
    out_ref[...] = scatter(idx_ref, value_ref, from_ref, to_ref, total)


def sweep_up_kernel(
    sum_ref, area_ref, e_ref, g_ref, f_ref, value_ref, idx_ref, out_ref, own_ref, held_ref, from_ref, to_ref, sems
):
    def half(n):
        rows = [pl.ds(n * 64 + v * 8, 8) for v in range(8)]
        value = [e_ref[0, r, :] + f_ref[r, :] * (sum_ref[r, :] / area_ref[r, :]) for r in rows]
        for level in range(LEVELS):
            i, s = divmod(level, 8)
            for v, r in enumerate(rows):
                if level:
                    value[v] = e_ref[level, r, :] + g_ref[level, r, :] * value[v]
                held_ref[i, pl.ds(n * 512 + v * 64 + s, 8, stride=8), :] = value[v]
        part = pl.ds(n * 512, 512)
        return pltpu.make_async_copy(held_ref.at[:, part, :], out_ref.at[:, part, :], sems.at[n])

    copies = []
    for n in range(2):
        copies.append(half(n))
        copies[-1].start()
    place = lambda slot: SLOTS.index(slot) * ROWS
    total = list_chunks(from_ref, to_ref, 0, True, place, SPARE, slots=SLOTS[-1:])
    own_ref[...] = scatter(idx_ref, value_ref, from_ref, to_ref, total)
    for copy in copies:
        copy.wait()


def ocean_scatter_kernel(
    a_ref, b_ref, minus_ref, plus_ref, own_ref, idx_ref, temp_ref, warm_ref, resp_ref, mask_ref, area_ref,
    out_ref, value_ref, from_ref, to_ref,
):
    row = lax.axis_index("lat")
    places = {"C-": (minus_ref, 2), "C+": (plus_ref, 2)}
    for n, hop in enumerate("-0+"):
        places["A" + hop] = a_ref, n
        places["B" + hop] = b_ref, n
    for n, slot in enumerate(SLOTS[:-1]):
        in_ref, at = places[slot]
        value_ref[pl.ds(n * ROWS, ROWS), :] = in_ref[at]
    value_ref[pl.ds(SPARE, STEP), :] = jnp.zeros((STEP, 128), F32)
    place = lambda slot: SLOTS.index(slot) * ROWS
    total = list_chunks(from_ref, to_ref, row, True, place, SPARE, slots=SLOTS[:-1])
    flux = (scatter(idx_ref, value_ref, from_ref, to_ref, total) + own_ref[...]) / area_ref[...]
    gsea = resp_ref[...] * mask_ref[...].astype(F32)
    out_ref[...] = temp_ref[...] + gsea * (warm_ref[...] - flux)


def to_tiles(x):
    return x.reshape(4, 8, 128, 128).transpose(0, 2, 1, 3).reshape(4, 1024, 128)


def from_tiles(x):
    return x.reshape(4, 128, 8, 128).transpose(0, 2, 1, 3).reshape(LEVELS, 16384)


BOTH = ("lat", "lon")


def swap_rows(x):
    return lax.ppermute(x, BOTH, [(i * 16 + j, (i ^ 1) * 16 + j) for i in range(8) for j in range(16)])


def outer_rows(x):
    pairs = []
    for i in range(8):
        to = i + 1 if i % 2 else i - 1
        for j in range(16):
            if 0 <= to < 8:
                pairs.append((i * 16 + j, to * 16 + j))
            elif i == 7:
                pairs.append((i * 16 + j, i * 16 + (j + 8) % 16))
    return lax.ppermute(x, BOTH, pairs)


def along_row(x, hop):
    return lax.ppermute(x, "lon", [(j, (j + hop) % 16) for j in range(16)])


def held(*dims, dtype=F32):
    return pltpu.VMEM(dims, dtype)


def call(kernel, outs, args, scratch=(), from_hbm=()):
    scalar = [x.dtype == jnp.int32 and x.shape[0] == 1 for x in args]
    place = lambda x, is_scalar: x if is_scalar else pltpu.with_memory_space_constraint(x, pltpu.VMEM)
    specs = [HBM if isinstance(x, jax.ShapeDtypeStruct) and len(x.shape) == 3 else VMEM for x in outs]
    return pl.pallas_call(
        kernel,
        out_shape=outs,
        in_specs=[HBM] * len(from_hbm) + [SMEM if s else VMEM for s in scalar],
        out_specs=specs,
        scratch_shapes=list(scratch),
        compiler_params=pltpu.CompilerParams(vmem_limit_bytes=8 << 20),
        name=kernel.__name__,
    )(*[pltpu.with_memory_space_constraint(x, pltpu.HBM) for x in from_hbm], *[place(x, s) for x, s in zip(args, scalar)])


def on_device(
    lower, upper, old_temp, atm_area, pair_count, cell_column, exchange_cell_weight, cell_coef, cell_ocean,
    surface_temp, extra_warming, response, sea_mask, ocean_area,
):
    square = lambda x: x.reshape(128, 128)
    cells = lambda x: x.reshape(10 * ROWS, 128)
    table = pltpu.VMEM((2, 128, 256), BF16)

    sources = [square(x) for x in (surface_temp, extra_warming, response, sea_mask)] + [cells(cell_ocean)]
    sources += [to_tiles(x) for x in (lower, upper, old_temp)]
    sources += [cells(x) for x in (cell_column, exchange_cell_weight, cell_coef)]
    sources += [square(x) for x in (atm_area, ocean_area)]
    *kept, sent = call(
        ocean_gather_kernel,
        [held(*x.shape, dtype=x.dtype) for x in sources] + [held(2 * SPARE + 2 * ROWS, 128)],
        [],
        [table, *LIST, pltpu.SemaphoreType.DMA((len(sources),))],
        sources,
    )
    ocean, (low, up, old), (columns, weight, coef), (atm_area, ocean_area) = kept[:5], kept[5:8], kept[8:11], kept[11:]
    a = swap_rows(sent[: 6 * ROWS].reshape(3, 2, ROWS, 128))
    b = outer_rows(sent[6 * ROWS : 12 * ROWS].reshape(3, 2, ROWS, 128))
    c = sent[12 * ROWS : 16 * ROWS].reshape(2, 2, ROWS, 128)

    e, g, f, own = call(
        sweep_down_kernel,
        [held(LEVELS, 128, 128), held(LEVELS, 128, 128), held(128, 128), held(2 * ROWS + 2 * ROWS, 128)],
        [low, up, old, *ocean],
        [table, *LIST],
    )
    a, b, f = lax.optimization_barrier((a, b, f))
    minus = along_row(jnp.stack([a[0], b[0], c[0]]), 1)
    plus = along_row(jnp.stack([a[2], b[2], c[1]]), -1)

    (at_columns,) = call(
        column_gather_kernel, [held(2 * (SPARE + STEP), 128)], [pair_count, e, f, columns], [table, *LIST]
    )
    (weighted,) = call(
        flux_kernel, [held(SPARE + STEP, 128)], [pair_count, minus, plus, a, b, own, at_columns, coef, weight]
    )
    minus, plus, middle = [weighted[n * 3 * ROWS : (n + 1) * 3 * ROWS].reshape(3, ROWS, 128) for n in range(3)]
    minus, plus = along_row(minus, -1), along_row(plus, 1)

    (sums,) = call(column_scatter_kernel, [held(128, 128)], [pair_count, weighted, columns], LIST)
    minus, plus, sums = lax.optimization_barrier((minus, plus, sums))
    a = swap_rows(jnp.stack([minus[0], middle[0], plus[0]]))
    b = outer_rows(jnp.stack([minus[1], middle[1], plus[1]]))

    level_warmth_new, own = call(
        sweep_up_kernel,
        [jax.ShapeDtypeStruct((4, 1024, 128), F32), held(128, 128)],
        [sums, atm_area, e, g, f, weighted, ocean[4]],
        [held(4, 1024, 128), *LIST, pltpu.SemaphoreType.DMA((2,))],
    )
    (fresh_seawater_warmth,) = call(
        ocean_scatter_kernel,
        [jax.ShapeDtypeStruct((128, 128), F32)],
        [a, b, minus, plus, own, ocean[4], *ocean[:4], ocean_area],
        [held(SPARE + STEP, 128), *LIST],
    )
    return from_tiles(level_warmth_new), fresh_seawater_warmth.reshape(16384)


def solution(mesh):
    owners = ("lat", "lon")
    wide, flat = P(None, owners), P(owners)
    lists = P(owners, None, None)
    body = jax.shard_map(
        on_device,
        mesh=mesh,
        in_specs=(wide, wide, wide, flat, P(owners, None), lists, lists, lists, lists) + (flat,) * 5,
        out_specs=(wide, flat),
        check_vma=False,
    )
    return body
```

```python
import functools

import jax
import jax.numpy as jnp
from jax import lax
from jax.experimental import pallas as pl
from jax.experimental.pallas import tpu as pltpu
from jax.sharding import PartitionSpec as P

F32 = jnp.float32
BF16 = jnp.bfloat16
ROWS = 32
STEP = 8
CHUNKS = ROWS // STEP
UNROLL = 4
LEVELS = 32
SPARE = 9 * ROWS
BLOCK = ROWS + STEP
VMEM = pl.BlockSpec(memory_space=pltpu.VMEM)
SMEM = pl.BlockSpec(memory_space=pltpu.SMEM)
HBM = pl.BlockSpec(memory_space=pltpu.HBM)

SLOTS = ("A-", "A0", "A+", "B-", "B0", "B+", "C-", "C+", "C0")
FAR, NEAR = SLOTS[:6], SLOTS[6:]
STAY, MOVE = ("A0", "B0", "C0"), ("A-", "B-", "C-", "A+", "B+", "C+")


def slot_kind(slot, row, ocean):
    hop = "-0+".index(slot[1])
    if slot[0] == "C":
        return 3 + hop, True
    below = (lax.rem(row, 2) == 1) == (ocean == (slot[0] == "A"))
    kind = jnp.where(below, 6, 0) + hop
    if slot[0] == "A":
        return kind, True
    if hop == 1:
        return jnp.where(row == 7, 9, kind), row > 0
    return kind, (row > 0) & (row < 7)


def list_chunks(from_ref, to_ref, row, ocean, place, spare, count_ref=None, slots=SLOTS):
    total = jnp.int32(0)
    for slot in slots:
        kind, exists = slot_kind(slot, row, ocean)
        number = CHUNKS
        if count_ref is not None:
            count = count_ref(slot) if callable(count_ref) else count_ref[0, kind]
            number = lax.div(count + (STEP * 128 - 1), STEP * 128)
        for c in range(CHUNKS):
            from_ref[total + c] = kind * ROWS + c * STEP
            to_ref[total + c] = place(slot) + c * STEP
        total = total + jnp.where(exists, number, 0)
    for c in range(2 * UNROLL):
        from_ref[total + c] = jnp.int32(0)
        to_ref[total + c] = jnp.int32(spare)
    return total


LIST = [pltpu.SMEM((9 * CHUNKS + 2 * UNROLL,), jnp.int32)] * 2
TRIPS = lambda total: lax.div(total + (UNROLL - 1), UNROLL)


def rows_at(start):
    return pl.ds(pl.multiple_of(start, STEP), STEP)


def spread(x, r, n):
    return jnp.broadcast_to(x[r : r + 1], (n, 128))


def two_terms(x):
    high = x.astype(BF16)
    return high, (x - high.astype(F32)).astype(BF16)


def fill_table(table_ref, fields):
    for t, field in enumerate(fields):
        for p, term in enumerate(two_terms(field)):
            table_ref[p, pl.ds(t * 64, 64), 0:128] = term[0:64]
            table_ref[p, pl.ds(t * 64, 64), 128:256] = term[64:128]


def look_up(table_ref, idx, accs, iota):
    k = ((idx & 127) | ((idx >> 13) << 7)).astype(F32)
    one, zero = jnp.ones((), BF16), jnp.zeros((), BF16)
    for h, acc in enumerate(accs):
        hot = [jnp.where(iota == spread(k, r, 256).astype(BF16), one, zero) for r in (2 * h, 2 * h + 1)]
        pltpu.matmul_push_rhs(jnp.concatenate(hot, axis=1), h // 2, h % 2)
        pltpu.matmul_acc_lhs(acc, table_ref[0], load_staged_rhs=h // 2)
        pltpu.matmul_acc_lhs(acc, table_ref[1])


def pick(idx, accs):
    group, place = (idx >> 10) & 7, (idx >> 7) & 7
    iota = lax.broadcasted_iota(jnp.int32, (8, 128), 0)
    values = [None, None]
    for h, acc in enumerate(accs):
        found = pltpu.matmul_pop(acc)
        for r in range(2):
            row, cols = 2 * h + r, slice(r * 128, r * 128 + 128)
            here = spread(group, row, 8)
            for t in range(2):
                eight = found[t * 64 : t * 64 + 8, cols]
                for j in range(1, 8):
                    eight = jnp.where(here == j, found[t * 64 + 8 * j : t * 64 + 8 * j + 8, cols], eight)
                value = jnp.take_along_axis(eight, spread(place, row, 8), axis=0)
                values[t] = value if row == 0 else jnp.where(iota == row, value, values[t])
    return values


def gather(table_ref, idx_ref, out_ref, apart, from_ref, to_ref, total):
    def run(*accs):
        iota = lax.broadcasted_iota(jnp.int32, (256, 128), 0).astype(F32).astype(BF16)
        sets = accs[:4], accs[4:]
        read = lambda n: idx_ref[rows_at(from_ref[n]), :]

        def finish(n, which):
            for t, value in enumerate(pick(read(n), sets[which])):
                out_ref[rows_at(to_ref[n] + t * apart), :] = value

        look_up(table_ref, read(0), sets[0], iota)

        def body(trip, _):
            for u in range(UNROLL):
                n = trip * UNROLL + u
                look_up(table_ref, read(n + 1), sets[(u + 1) % 2], iota)
                finish(n, u % 2)
            return 0

        lax.fori_loop(0, TRIPS(total), body, 0)
        for acc in sets[0]:
            pltpu.matmul_pop(acc)

    pl.run_scoped(run, *[pltpu.ACC(h % 2)((128, 256), F32) for _ in range(2) for h in range(4)])


def scatter(idx_ref, value_ref, from_ref, to_ref, total):
    def run(acc0, acc1):
        accs = acc0, acc1
        iota = lax.broadcasted_iota(jnp.int32, (128, 128), 0).astype(F32).astype(BF16)
        one, zero = jnp.ones((), BF16), jnp.zeros((), BF16)

        def body(trip, _):
            for u in range(UNROLL):
                n = trip * UNROLL + u
                idx = idx_ref[rows_at(from_ref[n]), :]
                value = value_ref[rows_at(to_ref[n]), :]
                low, high = (idx & 127).astype(F32), (idx >> 7).astype(F32)
                first = value.astype(BF16).astype(F32)
                second = value - first
                for h in range(4):
                    left, right = [], [[], []]
                    for r in (2 * h, 2 * h + 1):
                        at = lambda x: spread(x, r, 128).astype(BF16)
                        left.append(jnp.where(iota == at(high), one, zero))
                        mask = iota == at(low)
                        right[0].append(jnp.where(mask, at(first), zero))
                        right[1].append(jnp.where(mask, at(second), zero))
                    ahead = h >= 2
                    if ahead:
                        right = [[x.T for x in side] for side in zip(*right)]
                    right = jnp.concatenate([jnp.concatenate(x, axis=1) for x in right], axis=0)
                    pltpu.matmul_push_rhs(right, h // 2, h % 2, transpose=not ahead)
                    pltpu.matmul_acc_lhs(accs[h % 2], jnp.concatenate(left, axis=1), load_staged_rhs=h // 2)
            return 0

        lax.fori_loop(0, TRIPS(total), body, 0)
        both = pltpu.matmul_pop(acc0) + pltpu.matmul_pop(acc1)
        return both[:, 0:128] + both[:, 128:256]

    return pl.run_scoped(run, *[pltpu.ACC(m)((128, 256), F32) for m in range(2)])


def ocean_gather_kernel(*refs):
    count = (len(refs) - 5) // 2
    sources, kept = refs[:count], refs[count : 2 * count]
    out_ref, table_ref, from_ref, to_ref, sems = refs[2 * count :]
    copies = [pltpu.make_async_copy(x, y, sems.at[n]) for n, (x, y) in enumerate(zip(sources, kept))]
    for copy in copies:
        copy.start()
    for copy in copies[:5]:
        copy.wait()
    gather_ocean(kept[:5], out_ref, table_ref, from_ref, to_ref, FAR)
    for copy in copies[5:]:
        copy.wait()


def gather_ocean(fields, out_ref, table_ref, from_ref, to_ref, slots):
    place = lambda slot: slots.index(slot) * 2 * ROWS
    total = list_chunks(from_ref, to_ref, lax.axis_index("lat"), True, place, len(slots) * 2 * ROWS, slots=slots)
    fill_table(table_ref, ocean_states(*fields[:4]))
    gather(table_ref, fields[4], out_ref, ROWS, from_ref, to_ref, total)


def ocean_states(temp_ref, warm_ref, resp_ref, mask_ref):
    gsea = resp_ref[...] * mask_ref[...].astype(F32)
    return temp_ref[...] + gsea * warm_ref[...], gsea


def sweep_down_kernel(low_ref, up_ref, old_ref, *refs):
    fields, (e_ref, g_ref, f_ref, out_ref, table_ref, from_ref, to_ref) = refs[:5], refs[5:]

    def half(n, _):
        e = [jnp.zeros((8, 128), F32) for _ in range(8)]
        g = [jnp.zeros((8, 128), F32) for _ in range(8)]
        for level in range(LEVELS - 1, -1, -1):
            i, s = divmod(level, 8)
            for v in range(8):
                at = pl.ds(n * 512 + v * 64 + s, 8, stride=8)
                to = rows_at(n * 64 + v * 8)
                low, up, old = low_ref[i, at, :], up_ref[i, at, :], old_ref[i, at, :]
                inverse = 1.0 / (1.0 + low + up - up * g[v])
                e[v] = (old + up * e[v]) * inverse
                e_ref[level, to, :] = e[v]
                if level:
                    g[v] = low * inverse
                    g_ref[level, to, :] = g[v]
                else:
                    f_ref[to, :] = inverse
        return 0

    lax.fori_loop(0, 2, half, 0)
    gather_ocean(fields, out_ref, table_ref, from_ref, to_ref, NEAR)


def column_gather_kernel(count_ref, e_ref, f_ref, column_ref, out_ref, table_ref, from_ref, to_ref):
    fill_table(table_ref, (e_ref[0], f_ref[...]))
    place = lambda slot: SLOTS.index(slot) * ROWS
    total = list_chunks(from_ref, to_ref, lax.axis_index("lat"), False, place, SPARE, count_ref)
    gather(table_ref, column_ref, out_ref, SPARE + STEP, from_ref, to_ref, total)


def flux_kernel(count_ref, minus_ref, plus_ref, a_ref, b_ref, own_ref, column_ref, coef_ref, weight_ref, out_ref):
    row = lax.axis_index("lat")
    places = {"A0": (a_ref, 1), "B0": (b_ref, 1), "C0": (own_ref, 2)}
    for n, side in enumerate("ABC"):
        places[side + "-"] = minus_ref, n
        places[side + "+"] = plus_ref, n
    order = lax.broadcasted_iota(jnp.int32, (ROWS, 128), 0) * 128 + lax.broadcasted_iota(
        jnp.int32, (ROWS, 128), 1
    )
    for n, slot in enumerate(SLOTS):
        in_ref, at = places[slot]
        state = in_ref[pl.ds(at * 2 * ROWS, 2 * ROWS), :]
        target, gsea = state[:ROWS], state[ROWS:]
        kind, exists = slot_kind(slot, row, False)
        count = jnp.where(exists, count_ref[0, kind], 0)
        rows = pl.ds(pl.multiple_of(kind * ROWS, ROWS), ROWS)
        coef = coef_ref[rows, :]
        e, f = column_ref[pl.ds(n * ROWS, ROWS), :], column_ref[pl.ds(SPARE + STEP + n * ROWS, ROWS), :]
        flux = coef * (target - e) / (1.0 + coef * (gsea + f))
        out_ref[pl.ds(n * BLOCK, ROWS), :] = jnp.where(order < count, weight_ref[rows, :] * flux, 0.0)
        out_ref[pl.ds(n * BLOCK + ROWS, STEP), :] = jnp.full((STEP, 128), count.astype(F32))
    out_ref[pl.ds(9 * BLOCK, STEP), :] = jnp.zeros((STEP, 128), F32)


def scatter_columns(count_ref, value_ref, idx_ref, from_ref, to_ref, slots):
    row = lax.axis_index("lat")
    place = lambda slot: SLOTS.index(slot) * BLOCK
    total = list_chunks(from_ref, to_ref, row, False, place, 9 * BLOCK, count_ref, slots)
    return scatter(idx_ref, value_ref, from_ref, to_ref, total)


def near_scatter_kernel(count_ref, value_ref, column_ref, out_ref, from_ref, to_ref):
    out_ref[...] = scatter_columns(count_ref, value_ref, column_ref, from_ref, to_ref, NEAR)


def scatter_ocean(blocks, value_ref, idx_ref, from_ref, to_ref):
    slots, counts = tuple(blocks), {}
    for n, (in_ref, first) in enumerate(blocks.values()):
        block = in_ref[pl.ds(first, BLOCK), :]
        value_ref[pl.ds(n * ROWS, ROWS), :] = block[:ROWS]
        counts[slots[n]] = block[ROWS, 0].astype(jnp.int32)
    spare = len(slots) * ROWS
    value_ref[pl.ds(spare, STEP), :] = jnp.zeros((STEP, 128), F32)
    place = lambda slot: slots.index(slot) * ROWS
    total = list_chunks(from_ref, to_ref, lax.axis_index("lat"), True, place, spare, counts.get, slots)
    return scatter(idx_ref, value_ref, from_ref, to_ref, total)


def sweep_up_kernel(
    count_ref, near_ref, area_ref, e_ref, g_ref, f_ref, value_ref, column_ref, a_ref, b_ref, idx_ref,
    out_ref, stay_ref, held_ref, sum_ref, part_ref, from_ref, to_ref, sems,
):
    sum_ref[...] = near_ref[...] + scatter_columns(count_ref, value_ref, column_ref, from_ref, to_ref, FAR)

    def half(n):
        rows = [pl.ds(n * 64 + v * 8, 8) for v in range(8)]
        value = [e_ref[0, r, :] + f_ref[r, :] * (sum_ref[r, :] / area_ref[r, :]) for r in rows]
        for level in range(LEVELS):
            i, s = divmod(level, 8)
            for v, r in enumerate(rows):
                if level:
                    value[v] = e_ref[level, r, :] + g_ref[level, r, :] * value[v]
                held_ref[i, pl.ds(n * 512 + v * 64 + s, 8, stride=8), :] = value[v]
        part = pl.ds(n * 512, 512)
        return pltpu.make_async_copy(held_ref.at[:, part, :], out_ref.at[:, part, :], sems.at[n])

    copies = []
    for n in range(2):
        copies.append(half(n))
        copies[-1].start()
    blocks = {"A0": (a_ref, BLOCK), "B0": (b_ref, BLOCK), "C0": (value_ref, 8 * BLOCK)}
    stay_ref[...] = scatter_ocean(blocks, part_ref, idx_ref, from_ref, to_ref)
    for copy in copies:
        copy.wait()


def ocean_scatter_kernel(
    minus_ref, plus_ref, stay_ref, idx_ref, temp_ref, warm_ref, resp_ref, mask_ref, area_ref,
    out_ref, part_ref, from_ref, to_ref,
):
    blocks = {slot: (plus_ref if slot[1] == "+" else minus_ref, n % 3 * BLOCK) for n, slot in enumerate(MOVE)}
    flux = (scatter_ocean(blocks, part_ref, idx_ref, from_ref, to_ref) + stay_ref[...]) / area_ref[...]
    gsea = resp_ref[...] * mask_ref[...].astype(F32)
    out_ref[...] = temp_ref[...] + gsea * (warm_ref[...] - flux)


def to_tiles(x):
    return x.reshape(4, 8, 128, 128).transpose(0, 2, 1, 3).reshape(4, 1024, 128)


def from_tiles(x):
    return x.reshape(4, 128, 8, 128).transpose(0, 2, 1, 3).reshape(LEVELS, 16384)


BOTH = ("lat", "lon")


def swap_rows(x):
    return lax.ppermute(x, BOTH, [(i * 16 + j, (i ^ 1) * 16 + j) for i in range(8) for j in range(16)])


def outer_rows(x):
    pairs = []
    for i in range(8):
        to = i + 1 if i % 2 else i - 1
        for j in range(16):
            if 0 <= to < 8:
                pairs.append((i * 16 + j, to * 16 + j))
            elif i == 7:
                pairs.append((i * 16 + j, i * 16 + (j + 8) % 16))
    return lax.ppermute(x, BOTH, pairs)


def along_row(up, down):
    moves = lambda hop: [(j, (j + hop) % 16) for j in range(16)]
    return lax.ppermute(up, "lon", moves(1)), lax.ppermute(down, "lon", moves(-1))


def held(*dims, dtype=F32):
    return pltpu.VMEM(dims, dtype)


def call(kernel, outs, args, scratch=(), from_hbm=()):
    scalar = [x.dtype == jnp.int32 and x.shape[0] == 1 for x in args]
    place = lambda x, is_scalar: x if is_scalar else pltpu.with_memory_space_constraint(x, pltpu.VMEM)
    specs = [HBM if isinstance(x, jax.ShapeDtypeStruct) and len(x.shape) == 3 else VMEM for x in outs]
    return pl.pallas_call(
        kernel,
        out_shape=outs,
        in_specs=[HBM] * len(from_hbm) + [SMEM if s else VMEM for s in scalar],
        out_specs=specs,
        scratch_shapes=list(scratch),
        compiler_params=pltpu.CompilerParams(vmem_limit_bytes=4 << 20),
        name=kernel.__name__,
    )(*[pltpu.with_memory_space_constraint(x, pltpu.HBM) for x in from_hbm], *[place(x, s) for x, s in zip(args, scalar)])


def on_device(
    lower, upper, old_temp, atm_area, pair_count, cell_column, exchange_cell_weight, cell_coef, cell_ocean,
    surface_temp, extra_warming, response, sea_mask, ocean_area,
):
    square = lambda x: x.reshape(128, 128)
    cells = lambda x: x.reshape(10 * ROWS, 128)
    table = pltpu.VMEM((2, 128, 256), BF16)

    sources = [square(x) for x in (surface_temp, extra_warming, response, sea_mask)] + [cells(cell_ocean)]
    sources += [to_tiles(x) for x in (lower, upper, old_temp)]
    sources += [cells(x) for x in (cell_column, exchange_cell_weight, cell_coef)]
    sources += [square(x) for x in (atm_area, ocean_area)]
    *kept, sent = call(
        ocean_gather_kernel,
        [held(*x.shape, dtype=x.dtype) for x in sources] + [held(14 * ROWS, 128)],
        [],
        [table, *LIST, pltpu.SemaphoreType.DMA((len(sources),))],
        sources,
    )
    ocean, (low, up, old), (columns, weight, coef), (atm_area, ocean_area) = kept[:5], kept[5:8], kept[8:11], kept[11:]
    a = swap_rows(sent[: 6 * ROWS])
    b = outer_rows(sent[6 * ROWS : 12 * ROWS])

    e, g, f, c = call(
        sweep_down_kernel,
        [held(LEVELS, 128, 128), held(LEVELS, 128, 128), held(128, 128), held(8 * ROWS, 128)],
        [low, up, old, *ocean],
        [table, *LIST],
    )
    a, b, f = lax.optimization_barrier((a, b, f))
    pair = lambda x, n: x[n * 2 * ROWS : (n + 1) * 2 * ROWS]
    minus, plus = along_row(
        jnp.concatenate([pair(a, 0), pair(b, 0), pair(c, 0)]), jnp.concatenate([pair(a, 2), pair(b, 2), pair(c, 1)])
    )

    (at_columns,) = call(
        column_gather_kernel,
        [held(2 * (SPARE + STEP), 128)],
        [pair_count, e, f, columns],
        [table, *LIST],
    )
    (weighted,) = call(
        flux_kernel, [held(9 * BLOCK + STEP, 128)], [pair_count, minus, plus, a, b, c, at_columns, coef, weight]
    )
    a, b = swap_rows(weighted[: 3 * BLOCK]), outer_rows(weighted[3 * BLOCK : 6 * BLOCK])

    (near,) = call(near_scatter_kernel, [held(128, 128)], [pair_count, weighted, columns], LIST)
    a, b, near = lax.optimization_barrier((a, b, near))
    block = lambda x, n: x[n * BLOCK : (n + 1) * BLOCK]
    plus, minus = along_row(
        jnp.concatenate([block(a, 2), block(b, 2), block(weighted, 7)]),
        jnp.concatenate([block(a, 0), block(b, 0), block(weighted, 6)]),
    )

    level_warmth_new, stay = call(
        sweep_up_kernel,
        [jax.ShapeDtypeStruct((4, 1024, 128), F32), held(128, 128)],
        [pair_count, near, atm_area, e, g, f, weighted, columns, a, b, ocean[4]],
        [held(4, 1024, 128), held(128, 128), held(3 * ROWS + STEP, 128), *LIST, pltpu.SemaphoreType.DMA((2,))],
    )
    (fresh_seawater_warmth,) = call(
        ocean_scatter_kernel,
        [jax.ShapeDtypeStruct((128, 128), F32)],
        [minus, plus, stay, ocean[4], *ocean[:4], ocean_area],
        [held(6 * ROWS + STEP, 128), *LIST],
    )
    return from_tiles(level_warmth_new), fresh_seawater_warmth.reshape(16384)


def solution(mesh):
    owners = ("lat", "lon")
    wide, flat = P(None, owners), P(owners)
    lists = P(owners, None, None)
    body = jax.shard_map(
        on_device,
        mesh=mesh,
        in_specs=(wide, wide, wide, flat, P(owners, None), lists, lists, lists, lists) + (flat,) * 5,
        out_specs=(wide, flat),
        check_vma=False,
    )
    return body
```
